256 devices in a mesh: tile: 32 (over y, z_hi, core), group: 8 (over z_lo, x).
Axes of the slice: x: 4, y: 4, z: 8 (z_hi: 4, z_lo: 2; z = z_hi * 2 + z_lo), core: 2. Of those that a mesh axis runs over, the one named last changes fastest.
Arguments:
- latents: bfloat16 [1536, 128, 1536], P(('tile', 'group')), may hold values from -6 to 6
- window_index: int32 [3072], P(('tile', 'group')), may hold values from 0 to 2039
- window_len: int32 [3072], P(('tile', 'group')), may hold values from 1 to 64
- live_blocks: int32 [256], P(('tile', 'group')), may hold values from 0 to 6, as said below
- norm_gain: float32 [1536], replicated, may hold values from 0.1 to 1.9
- w_qkv: bfloat16 [1536, 4608], P('group', 'tile'), may hold values from -0.15625 to 0.15625
- w_out: bfloat16 [1536, 1536], P('group', 'tile'), may hold values from -0.15625 to 0.15625
Outputs:
- refined: bfloat16 [1536, 128, 1536], P(('tile', 'group'))
The draws below stay inside these ranges and needn't reach their ends.
Inputs may be any that keep to these rules, and one draw needn't show every extreme that they name: `live_blocks`: the device at tile index i and the device at tile index i + 16 in the same group form a pair; at most one of a pair holds more than 4 live blocks, the two hold at most 8 together, and in every draw some pair holds exactly 6 and 2.
All inputs are finite; a program needn't handle non-finite values.
Results may differ from the reference program's by a relative error of at most 0.0033.
Values may be sent and summed in bfloat16 or wider, within the bound.
A program may use at most 128 MiB of HBM per device.

```python
import math
import jax
import jax.numpy as jnp
from jax import lax

D = 1536
HEADS = 24
HEAD_DIM = 64
WIN_SIDE = 8
WIN_ROWS = 34
WIN_COLS = 60
SLOTS = 6
CAP = 4
WIN_TOK = 64
BLOCK = 128
BLOCKS = 1536
WINDOWS = 3072
N_TILE = 32
N_GROUP = 8


def draw_window_len(key, part):
    key_full, key_part = jax.random.split(key, 2)
    full_pick = jax.random.randint(key_full, (WINDOWS,), 0, 5) < 3
    partial_len = jax.random.randint(key_part, (WINDOWS,), 1, WIN_TOK + 1)
    return jnp.where(full_pick, WIN_TOK, partial_len).astype(jnp.int32)


def draw_live_blocks(key, part):
    half_tiles = N_TILE // 2
    key_hot, key_cold, key_flip = jax.random.split(key, 3)
    heavy = jax.random.randint(key_hot, (half_tiles, N_GROUP), CAP, SLOTS + 1)
    heavy = heavy.at[0, 0].set(SLOTS)
    spare_room = 2 * CAP - heavy
    light = jax.random.randint(key_cold, (half_tiles, N_GROUP), 0, 1048576) % (spare_room + 1)
    light = light.at[0, 0].set(2 * CAP - SLOTS)
    flipped = jax.random.randint(key_flip, (half_tiles, N_GROUP), 0, 2) == 1
    lower = jnp.where(flipped, heavy, light)
    upper = jnp.where(flipped, light, heavy)
    return jnp.concatenate([lower, upper], axis=0).reshape(N_TILE * N_GROUP).astype(jnp.int32)


def set_ends(drawn, key, smallest, high):
    shape = drawn.shape
    place = [jax.random.randint(jax.random.fold_in(key, axis), (), 0, shape[axis]) for axis in range(len(shape))]
    drawn = drawn.at[tuple(place)].set(smallest)
    longest = shape.index(max(shape))
    place[longest] = (place[longest] + 1) % shape[longest]
    return drawn.at[tuple(place)].set(high)


def block_scale(stream_key, extent, cuts, low, top_value):
    def one(axis_at, shards_of):
        steps = jax.random.uniform(jax.random.fold_in(jax.random.fold_in(stream_key, 6), axis_at), (shards_of,), jnp.float32, low / len(cuts), top_value / len(cuts))
        return jnp.repeat(jnp.exp(steps), extent[axis_at] // shards_of).reshape((-1,) + (1,) * (len(extent) - axis_at - 1))

    level = one(*cuts[0])
    for cut in cuts[1:]:
        level = level * one(*cut)
    return level


def normal_values(stream_key, shape, deviation, reach, shards=(), kind=jnp.bfloat16):
    gain = block_scale(stream_key, shape, shards, -0.22, 0.18) if shards else 1.0
    result = jax.random.normal(stream_key, shape, jnp.float32) * deviation * gain
    return jnp.minimum(jnp.maximum(result, -reach), reach).astype(kind)


def setup_inputs(seed: int = 0) -> dict:
    seeds = jax.random.split(jax.random.key(seed), 8)
    return {
        "latents": normal_values(seeds[0], (BLOCKS, BLOCK, D), 1.0, 6.0, ((0, 256),)),
        "window_index": set_ends(jax.random.randint(seeds[1], (WINDOWS,), 0, WIN_ROWS * WIN_COLS), jax.random.fold_in(seeds[1], 1), 0, (WIN_ROWS * WIN_COLS) - 1).astype(jnp.int32),
        "window_len": draw_window_len(jax.random.fold_in(seeds[7], 71), 0),
        "live_blocks": draw_live_blocks(jax.random.fold_in(seeds[7], 71), 0),
        "norm_gain": jnp.clip(1.0 + 0.18 * jax.random.normal(seeds[4], (D,), jnp.float32), 0.1, 1.9),
        "w_qkv": normal_values(seeds[5], (D, 3 * D), D ** -0.5, 0.15625, ((0, 8), (1, 32))),
        "w_out": normal_values(seeds[6], (D, D), D ** -0.5, 0.15625, ((0, 8), (1, 32))),
    }


def position_table(window_ids):
    token_ids = jnp.arange(WIN_TOK, dtype=jnp.int32)
    row_pos = window_ids[:, None] // WIN_COLS * WIN_SIDE + token_ids[None, :] // WIN_SIDE
    col_pos = window_ids[:, None] % WIN_COLS * WIN_SIDE + token_ids[None, :] % WIN_SIDE
    quarter = D // 4
    frequency = jnp.exp(jnp.arange(quarter, dtype=jnp.float32) * (-math.log(10000.0) / quarter))
    row_angle = row_pos.astype(jnp.float32)[:, :, None] * frequency
    col_angle = col_pos.astype(jnp.float32)[:, :, None] * frequency
    return jnp.concatenate([jnp.sin(row_angle), jnp.cos(row_angle), jnp.sin(col_angle), jnp.cos(col_angle)], axis=-1)

def head_norm(values):
    return (values * lax.rsqrt(lax.optimization_barrier(jnp.mean(values * values, axis=-1, keepdims=True)) + 1e-06)).astype(jnp.bfloat16)

def window_layer(blocks_in, window_ids, window_lens, norm_gain, w_qkv, w_out):
    window_count = window_ids.shape[0]
    stream = blocks_in.reshape(window_count, WIN_TOK, D).astype(jnp.float32) + position_table(window_ids)
    scale = lax.rsqrt(lax.optimization_barrier(jnp.mean(stream * stream, axis=-1, keepdims=True)) + 1e-06)
    normed = (stream * scale * norm_gain.astype(jnp.float32)).astype(jnp.bfloat16).reshape(window_count * WIN_TOK, D)
    projected = jnp.dot(normed, w_qkv, preferred_element_type=jnp.float32)
    projected = projected.reshape(window_count, WIN_TOK, 3, HEADS, HEAD_DIM)
    queries = head_norm(projected[:, :, 0])
    keys = head_norm(projected[:, :, 1])
    values = projected[:, :, 2].astype(jnp.bfloat16)
    scores = jnp.einsum('wqhd,wkhd->whqk', queries.astype(jnp.float32), keys.astype(jnp.float32)) * HEAD_DIM ** (-0.5)
    key_mask = jnp.arange(WIN_TOK, dtype=jnp.int32)[None, :] < window_lens[:, None]
    weights = jnp.exp(scores) * key_mask[:, None, None, :].astype(jnp.float32)
    probs = (weights / lax.optimization_barrier(jnp.sum(weights, axis=-1, keepdims=True))).astype(jnp.bfloat16)
    attended = jnp.einsum('whqk,wkhd->wqhd', probs.astype(jnp.float32), values.astype(jnp.float32))
    attended = attended.astype(jnp.bfloat16).reshape(window_count * WIN_TOK, D)
    update = jnp.dot(attended, w_out, preferred_element_type=jnp.float32)
    base = blocks_in.reshape(window_count * WIN_TOK, D).astype(jnp.float32)
    token_live = key_mask.reshape(window_count * WIN_TOK)[:, None]
    return jnp.where(token_live, base + update, base).astype(jnp.bfloat16).reshape(blocks_in.shape)

def reference(latents, window_index, window_len, live_blocks, norm_gain, w_qkv, w_out):
    device_count = BLOCKS // SLOTS

    def one_device(inputs):
        blocks_in, window_ids, window_lens, live_count = inputs
        finished = window_layer(blocks_in, window_ids, window_lens, norm_gain, w_qkv, w_out)
        slot_live = jnp.arange(SLOTS, dtype=jnp.int32) < live_count
        return jnp.where(slot_live[:, None, None], finished, blocks_in)
    refined = lax.map(one_device, (latents.reshape(device_count, SLOTS, BLOCK, D), window_index.reshape(device_count, 2 * SLOTS), window_len.reshape(device_count, 2 * SLOTS), live_blocks))
    return refined.reshape(BLOCKS, BLOCK, D)
```

```python
import math
import heapq

import jax
import jax.numpy as jnp
from jax import lax
from jax.experimental import pallas as pl
from jax.experimental.pallas import tpu as pltpu
from jax.sharding import PartitionSpec as P

D = 1536
HEAD_DIM = 64
WIN_SIDE = 8
WIN_COLS = 60
WIN_TOK = 64
SLOTS = 6
BLOCK = 128
TOK = SLOTS * BLOCK
PART = 96
LANES = 128
FULL = "F"
AXLEN = {"x": 4, "y": 4, "z": 8}
AXPOS = {"x": 0, "y": 1, "z": 2}
MESH = pl.DeviceIdType.MESH


def moved(region, axis, step):
    pos = AXPOS[axis]
    n = AXLEN[axis]
    out = list(region)
    out[pos] = (region[pos] - step) % n
    return tuple(out)

def plan():
    rate = 46.5e3
    free = {}
    queue = []
    order = []
    have = {}
    count = [0]
    seq = [0]

    def bytes_of(color, region, half):
        n = PART * 256
        for r in region:
            if r == FULL:
                n *= 4
        return n // 2 if half else n

    def send(now, color, region, axis, step, half=None):
        n = AXLEN[axis]
        hops = min(step, n - step)
        sign = 1 if step <= n // 2 else -1
        link = (axis, sign)
        start = max(now, free.get(link, 0.0))
        end = start + hops * bytes_of(color, region, half) / rate
        free[link] = end
        ident = count[0]
        count[0] += 1
        seq[0] += 1
        heapq.heappush(queue, (end + 1.0 + 0.75 * hops, seq[0], ident, color, moved(region, axis, step), half))
        return (ident, color, region, axis, step, half)

    def complete(now, color, region, out):
        rx, ry, rz = region
        if color == "A":
            if region == (0, 0, 0):
                for s in (1, 3, 2):
                    out.append(send(now, "A", region, "x", s))
                return
            if rz == 0 and ry == 0 and rx != FULL:
                if all(((k, 0, 0) in have["A"]) for k in (1, 2, 3)):
                    complete(now, "A", (FULL, 0, 0), out)
                return
            if rz == 0:
                if ry == 0:
                    out.append(send(now, "A", region, "y", 1))
                    out.append(send(now, "A", region, "y", 3))
                elif ry == 3:
                    out.append(send(now, "A", region, "y", 1, 0))
                elif ry == 1:
                    out.append(send(now, "A", region, "y", 3, 1))
                out.append(send(now, "A", region, "z", 1))
                out.append(send(now, "A", region, "z", 7))
            elif rz >= 5:
                out.append(send(now, "A", region, "z", 1, 0 if rz == 5 else None))
            elif rz <= 3:
                out.append(send(now, "A", region, "z", 7, 1 if rz == 3 else None))
            have["A", rz] = have.get(("A", rz), 0) + 1
            if have["A", rz] == 4:
                out.append(("sib", "A", (FULL, FULL, rz)))
            return
        mid, last = ("y", "x") if color == "B" else ("x", "y")
        m, l = AXPOS[mid], AXPOS[last]
        if region[m] != FULL and region[l] == 0:
            if region[m] == 0:
                if rz == 0:
                    out.append(send(now, color, region, "z", 1))
                    out.append(send(now, color, region, "z", 7))
                elif rz in (7, 6) or (rz == 5 and color == "B"):
                    out.append(send(now, color, region, "z", 1))
                elif rz in (1, 2) or (rz == 3 and color == "C"):
                    out.append(send(now, color, region, "z", 7))
                out.append(send(now, color, region, mid, 1))
                out.append(send(now, color, region, mid, 3))
            elif region[m] == 3 and rz % 2 == 0:
                out.append(send(now, color, region, mid, 1))
            elif region[m] == 1 and rz % 2 == 1:
                out.append(send(now, color, region, mid, 3))
            parts = []
            for k in range(4):
                r = list(region)
                r[m] = k
                parts.append(tuple(r) in have[color])
            if all(parts):
                r = list(region)
                r[m] = FULL
                complete(now, color, tuple(r), out)
            return
        if region[l] == 0:
            out.append(send(now, color, region, last, 1))
            out.append(send(now, color, region, last, 3))
        elif region[l] == 3:
            out.append(send(now, color, region, last, 1, 0))
        elif region[l] == 1:
            out.append(send(now, color, region, last, 3, 1))
        key = (color, region[l])
        have[key] = have.get(key, 0) + 1
        if have[key] == 8:
            out.append(("sib", color, (region[0], region[1], FULL)))

    first = []
    for color in "BCA":
        have[color] = {(0, 0, 0)}
        complete(0.0, color, (0, 0, 0), first)
    order.append((None, first))
    end = 0.0
    while queue:
        now, _, ident, color, region, half = heapq.heappop(queue)
        end = now
        out = []
        if half is None:
            have[color].add(region)
            complete(now, color, region, out)
        else:
            got = have[color]
            got.add((region, half))
            if (region, 1 - half) in got:
                got.add(region)
                complete(now, color, region, out)
        order.append(((ident, color, region, half), out))
    return order, count[0], end

def parts_of(ref_f, ref_r, color):
    if color == "A":
        return ref_r
    return ref_f.at[pl.ds(0 if color == "B" else PART, PART), :]


def gather_weights(src_f, src_r, wf, wr, send_sem, recv_sem, sib_sem, loc_sem, meanwhile=None):
    tile = lax.axis_index("tile"); group = lax.axis_index("group")
    y = tile // 8; zh = (tile // 2) % 4; c = tile % 2
    zl = group // 4; x = group % 4
    z = zh * 2 + zl

    xs = [x] + [(x + k) % 4 for k in (1, 2, 3)]
    ys = [y] + [(y + k) % 4 for k in (1, 2, 3)]
    zs = [(zl, zh)] + [(((z + k) % 8) % 2, ((z + k) % 8) // 2) for k in range(1, 8)]

    def dev_of(axis, step):
        xx, yy, zz, cc = x, y, zs[0], c
        if axis == "x": xx = xs[step]
        if axis == "y": yy = ys[step]
        if axis == "z": zz = zs[step]
        if axis == "c": cc = 1 - c
        return (yy * 8 + zz[1] * 2 + cc, zz[0] * 4 + xx)
    table = {}
    def dev(axis, step):
        if (axis, step) not in table:
            table[axis, step] = dev_of(axis, step)
        return table[axis, step]

    bar = pltpu.get_barrier_semaphore()
    peers = [("x", 1), ("x", 3), ("x", 2), ("y", 1), ("y", 3), ("z", 1), ("z", 7), ("c", 1)]
    for p in peers:
        pl.semaphore_signal(bar, inc=1, device_id=dev(*p), device_id_type=MESH)
    pl.semaphore_wait(bar, len(peers))

    own_f = wf.at[zl, x, y, zh, c]
    own_r = wr.at[zl, x, y, zh, c]
    loc_f = pltpu.make_async_copy(src_f, own_f, loc_sem.at[0])
    loc_r = pltpu.make_async_copy(src_r, own_r, loc_sem.at[1])
    loc_f.start()
    loc_r.start()

    def view(color, region, half=None, core=None):
        rx, ry, rz = region
        part = pl.ds(0, 4) if half is None else pl.ds(2 * half, 2)
        ix = part if rx == FULL else xs[rx]
        iy = part if ry == FULL else ys[ry]
        iz = (pl.ds(0, 2), pl.ds(0, 4)) if rz == FULL else zs[rz]
        cc = c if core is None else core
        if color == "A":
            return wr.at[iz[0], ix, iy, iz[1], cc]
        return wf.at[iz[0], ix, iy, iz[1], cc, pl.ds(0 if color == "B" else PART, PART), :]

    order, total, end = plan()
    sends, sibs = [], []
    def issue(item):
        if item[0] == "sib":
            _, color, region = item
            i = len(sibs)
            ref = view(color, region)
            cp = pltpu.make_async_remote_copy(src_ref=ref, dst_ref=ref, send_sem=sib_sem.at[0, i], recv_sem=sib_sem.at[1, i],
                                              device_id=dev("c", 1), device_id_type=MESH)
            sibs.append((cp, color, region))
        else:
            ident, color, region, axis, step, half = item
            if region == (0, 0, 0):
                ref = parts_of(src_f, src_r, color)
                dst = parts_of(own_f, own_r, color)
            else:
                ref = dst = view(color, region, half)
            cp = pltpu.make_async_remote_copy(src_ref=ref, dst_ref=dst, send_sem=send_sem.at[ident], recv_sem=recv_sem.at[ident],
                                              device_id=dev(axis, step), device_id_type=MESH)
            sends.append(cp)
        cp.start()
    for n, (arrival, out) in enumerate(order):
        if arrival is not None:
            ident, color, region, half = arrival
            ref = view(color, region, half)
            pltpu.make_async_remote_copy(src_ref=ref, dst_ref=ref, send_sem=send_sem.at[ident], recv_sem=recv_sem.at[ident],
                                         device_id=dev("c", 1), device_id_type=MESH).wait_recv()
        for item in out:
            issue(item)
        if n == 0:
            loc_f.wait()
            loc_r.wait()
            if meanwhile is not None:
                meanwhile()
    for i, (cp, color, region) in enumerate(sibs):
        ref = view(color, region, None, 1 - c)
        pltpu.make_async_remote_copy(src_ref=ref, dst_ref=ref, send_sem=sib_sem.at[0, i], recv_sem=sib_sem.at[1, i],
                                     device_id=dev("c", 1), device_id_type=MESH).wait_recv()
    for cp in sends:
        cp.wait_send()
    for cp, _, _ in sibs:
        cp.wait_send()


def window_tables(window_index):
    side = jnp.arange(WIN_SIDE, dtype=jnp.int32)
    rows = (window_index // WIN_COLS * WIN_SIDE)[:, None] + side
    cols = (window_index % WIN_COLS * WIN_SIDE)[:, None] + side
    quarter = D // 4
    frequency = jnp.exp(jnp.arange(quarter, dtype=jnp.float32) * (-math.log(10000.0) / quarter))
    angle = jnp.stack([rows, cols]).astype(jnp.float32)[..., None] * frequency
    return jnp.concatenate([jnp.sin(angle), jnp.cos(angle)], axis=-1)


def norm_tokens(lat, tables, gain, xs_ref):
    def block(b, carry):
        for h in range(2):
            rows = pl.ds(pl.multiple_of(b * BLOCK + h * WIN_TOK, WIN_TOK), WIN_TOK)
            win = 2 * b + h
            tok = lat[rows, :].astype(jnp.float32)
            half = D // 2
            left = tok[:, :half].reshape(8, 8, half) + tables[0, win][:, None, :]
            right = tok[:, half:].reshape(8, 8, half) + tables[1, win][None]
            stream = jnp.concatenate([left.reshape(WIN_TOK, half), right.reshape(WIN_TOK, half)], axis=1)
            scale = lax.rsqrt(jnp.mean(stream * stream, axis=-1, keepdims=True) + 1e-06)
            xs_ref[rows, :] = (stream * scale * gain[...]).astype(jnp.bfloat16)
        return carry

    lax.fori_loop(0, SLOTS, block, 0)


def coords(t):
    return t // 8, (t // 2) % 4, t % 2


def unpack_rest(wr, wu):
    lane = lax.broadcasted_iota(jnp.int32, (PART, LANES), 1) < 64

    def one(t, carry):
        y, zh, c = coords(t)
        for j in range(4):
            zl, x = j // 2, (j % 2) * 2
            even = wr[zl, x, y, zh, c].astype(jnp.float32)
            odd = wr[zl, x + 1, y, zh, c].astype(jnp.float32)
            low = jnp.where(lane, even, odd).astype(jnp.bfloat16)
            high = pltpu.roll(jnp.where(lane, odd, even), 64, 1).astype(jnp.bfloat16)
            for i in range(6):
                wu[j, y, zh, c, 32 * i:32 * i + 16, :] = low[16 * i:16 * i + 16]
                wu[j, y, zh, c, 32 * i + 16:32 * i + 32, :] = high[16 * i:16 * i + 16]
        return carry

    lax.fori_loop(0, 32, one, 0)


def column_tile(wf, wu, groups):
    spots = []
    for t, r in groups:
        spots.append(coords(t) + (pl.ds(pl.multiple_of(r, 16), 16),))
    tiles = []
    for k in range(12):
        j, kind = k // 3, k % 3
        if kind == 1:
            pieces = [wu[j, y, zh, c, rows, :] for y, zh, c, rows in spots]
        else:
            zl, x = j // 2, (j % 2) * 2 + kind // 2
            pieces = [wf[zl, x, y, zh, c, rows, :] for y, zh, c, rows in spots]
        tiles.append(jnp.concatenate(pieces, axis=0))
    return jnp.concatenate(tiles, axis=1)


NT = (((1,), (1,)), ((), ()))


def project(xs_ref, wf, wu, qkv):
    r = lax.broadcasted_iota(jnp.int32, (256, 256), 0) // HEAD_DIM
    c = lax.broadcasted_iota(jnp.int32, (256, 256), 1) // HEAD_DIM
    ones = jnp.where(r == c, 1.0, 0.0).astype(jnp.bfloat16)

    def tile(n, carry):
        groups = []
        for i in range(16):
            g = n * 16 + i
            groups.append((g // 9, (g % 9) * 16))
        p = lax.dot_general(xs_ref[...], column_tile(wf, wu, groups), NT, preferred_element_type=jnp.float32)
        total = jnp.dot((p * p).astype(jnp.bfloat16), ones, preferred_element_type=jnp.float32)
        extra = jnp.where(n < 6, HEAD_DIM ** -0.5, 1.0)
        factor = jnp.where(n < 12, lax.rsqrt(total * (1.0 / HEAD_DIM) + 1e-06) * extra, 1.0)
        qkv[n] = (p * factor).astype(jnp.bfloat16)
        return carry

    lax.fori_loop(0, 18, tile, 0)


def attend(qkv, lens, att):
    lane = lax.broadcasted_iota(jnp.int32, (BLOCK, LANES), 1) < 64
    key = lax.broadcasted_iota(jnp.int32, (BLOCK, 256), 1) % BLOCK
    query = lax.broadcasted_iota(jnp.int32, (BLOCK, 256), 0)
    one = jnp.where(lane, 1.0, 0.0).astype(jnp.bfloat16)
    sums = jnp.concatenate([one, 1.0 - one], axis=0).astype(jnp.bfloat16)

    def block(b, carry):
        rows = pl.ds(pl.multiple_of(b * BLOCK, BLOCK), BLOCK)
        first, second = lens[2 * b], lens[2 * b + 1]
        low = jnp.where(query < 64, 0, 64)
        high = jnp.where(query < 64, first, 64 + second)
        mask = jnp.where(key >= low, 1.0, 0.0) * jnp.where(key < high, 1.0, 0.0)

        def pair(h, inner):
            for part in range(2):
                cols = slice(part * LANES, part * LANES + LANES)
                q = qkv[h, rows, cols]
                k = qkv[6 + h, rows, cols]
                v = qkv[12 + h, rows, cols]
                zero = jnp.zeros_like(k)
                keys = jnp.concatenate([jnp.where(lane, k, zero), jnp.where(lane, zero, k)], axis=0)
                vals = jnp.concatenate([jnp.where(lane, v, zero), jnp.where(lane, zero, v)], axis=0)
                scores = lax.dot_general(q, keys, NT, preferred_element_type=jnp.float32)
                weights = (jnp.exp(scores) * mask).astype(jnp.bfloat16)
                mixed = jnp.dot(weights, jnp.concatenate([vals, sums], axis=1), preferred_element_type=jnp.float32)
                att[h, rows, cols] = (mixed[:, :LANES] / mixed[:, LANES:]).astype(jnp.bfloat16)
            return inner

        lax.fori_loop(0, 6, pair, 0)
        return carry

    lax.fori_loop(0, SLOTS, block, 0)


def finish(att, wf, wu, lat, lens, live, out):
    tok = lax.broadcasted_iota(jnp.int32, (BLOCK, 256), 0)

    def tile(n, carry):
        groups = []
        for i in range(16):
            g = n * 16 + i
            groups.append((g // 3, 144 + (g % 3) * 16))
        wide = jnp.concatenate([att[h] for h in range(6)], axis=1)
        update = lax.dot_general(wide, column_tile(wf, wu, groups), NT, preferred_element_type=jnp.float32)
        cols = pl.ds(pl.multiple_of(n * 256, 256), 256)
        for b in range(SLOTS):
            base = lat[b * BLOCK:(b + 1) * BLOCK, cols].astype(jnp.float32)
            first, second = lens[2 * b], lens[2 * b + 1]
            limit = jnp.where(tok < 64, first, 64 + second)
            limit = jnp.where(b < live[0], limit, 0)
            moved_rows = update[b * BLOCK:(b + 1) * BLOCK]
            out[b * BLOCK:(b + 1) * BLOCK, cols] = jnp.where(tok < limit, base + moved_rows, base).astype(jnp.bfloat16)
        return carry

    lax.fori_loop(0, 6, tile, 0)


def pack(w_qkv, w_out):
    cols = jnp.concatenate([w_qkv.T, w_out.T], axis=0)
    odd = lax.axis_index("group") % 2 == 1
    main = jnp.where(odd, cols[:, 64:], cols[:, :128])
    rest = jnp.where(odd, cols[:, :64], cols[:, 128:]).reshape(6, 2, 16, 64)
    rest = jnp.where(odd, rest[:, ::-1], rest)
    return main, jnp.concatenate([rest[:, 0], rest[:, 1]], axis=-1).reshape(PART, LANES)


WF = (2, 4, 4, 4, 2, 192, LANES)
WR = (2, 4, 4, 4, 2, PART, LANES)
WU = (4, 4, 4, 2, 192, LANES)
QKV = (18, TOK, 256)


def comm_sems():
    total = plan()[1]
    dma = pltpu.SemaphoreType.DMA
    return [dma((total,)), dma((total,)), dma((2, 16)), dma((2,))]


def gather_call(main, rest):
    return pl.pallas_call(
        gather_weights,
        out_shape=(jax.ShapeDtypeStruct(WF, jnp.bfloat16), jax.ShapeDtypeStruct(WR, jnp.bfloat16)),
        in_specs=[pl.BlockSpec(memory_space=pl.ANY)] * 2,
        out_specs=(pl.BlockSpec(memory_space=pl.ANY),) * 2,
        scratch_shapes=comm_sems(),
        compiler_params=pltpu.CompilerParams(collective_id=0, has_side_effects=True),
    )(main, rest)


def layer_kernel(lens, live, lat, tables, gain, wf_hbm, wr_hbm, out, wf, wr, wu, xs, qkv, att, sem):
    copies = [pltpu.make_async_copy(wr_hbm, wr, sem.at[0]), pltpu.make_async_copy(wf_hbm, wf, sem.at[1])]
    for copy in copies:
        copy.start()
    norm_tokens(lat, tables, gain, xs)
    copies[0].wait()
    unpack_rest(wr, wu)
    copies[1].wait()
    project(xs, wf, wu, qkv)
    attend(qkv, lens, att)
    finish(att, wf, wu, lat, lens, live, out)


def layer_call(lens, live, lat, tables, gain, wf, wr):
    smem = pl.BlockSpec(memory_space=pltpu.SMEM)
    vmem = pl.BlockSpec(memory_space=pltpu.VMEM)
    hbm = pl.BlockSpec(memory_space=pl.ANY)
    bf16 = jnp.bfloat16
    return pl.pallas_call(
        layer_kernel,
        out_shape=jax.ShapeDtypeStruct((TOK, D), bf16),
        in_specs=[smem, smem, vmem, vmem, vmem, hbm, hbm],
        out_specs=vmem,
        scratch_shapes=[pltpu.VMEM(WF, bf16), pltpu.VMEM(WR, bf16), pltpu.VMEM(WU, bf16), pltpu.VMEM((TOK, D), bf16),
                        pltpu.VMEM(QKV, bf16), pltpu.VMEM((6, TOK, 256), bf16), pltpu.SemaphoreType.DMA((2,))],
        compiler_params=pltpu.CompilerParams(vmem_limit_bytes=58 << 20),
    )(lens, live, lat, tables, gain, wf, wr)


def local(latents, window_index, window_len, live_blocks, norm_gain, w_qkv, w_out):
    main, rest = pack(w_qkv, w_out)
    wf, wr = gather_call(main, rest)
    out = layer_call(window_len, live_blocks, latents.reshape(TOK, D), window_tables(window_index),
                     norm_gain.reshape(1, D), wf, wr)
    return out.reshape(latents.shape)


def solution(mesh):
    in_specs = (
        P(("tile", "group"), None, None),
        P(("tile", "group")),
        P(("tile", "group")),
        P(("tile", "group")),
        P(),
        P("group", "tile"),
        P("group", "tile"),
    )
    out_specs = P(("tile", "group"), None, None)
    return jax.shard_map(local, mesh=mesh, in_specs=in_specs, out_specs=out_specs, check_vma=False)
```

```python
import math
import heapq

import jax
import jax.numpy as jnp
from jax import lax
from jax.experimental import pallas as pl
from jax.experimental.pallas import tpu as pltpu
from jax.sharding import PartitionSpec as P

D = 1536
HEAD_DIM = 64
WIN_SIDE = 8
WIN_COLS = 60
WIN_TOK = 64
SLOTS = 6
BLOCK = 128
TOK = SLOTS * BLOCK
PART = 96
LANES = 128
FULL = "F"
AXLEN = {"x": 4, "y": 4, "z": 8}
AXPOS = {"x": 0, "y": 1, "z": 2}
MESH = pl.DeviceIdType.MESH


def moved(region, axis, step):
    pos = AXPOS[axis]
    n = AXLEN[axis]
    out = list(region)
    out[pos] = (region[pos] - step) % n
    return tuple(out)

def plan():
    rate = 46.5e3
    free = {}
    queue = []
    order = []
    have = {}
    count = [0]
    seq = [0]

    def bytes_of(color, region, half):
        n = PART * 256
        for r in region:
            if r == FULL:
                n *= 4
        return n // 2 if half else n

    def send(now, color, region, axis, step, half=None):
        n = AXLEN[axis]
        hops = min(step, n - step)
        sign = 1 if step <= n // 2 else -1
        link = (axis, sign)
        start = max(now, free.get(link, 0.0))
        end = start + hops * bytes_of(color, region, half) / rate
        free[link] = end
        ident = count[0]
        count[0] += 1
        seq[0] += 1
        heapq.heappush(queue, (end + 1.0 + 0.75 * hops, seq[0], ident, color, moved(region, axis, step), half))
        return (ident, color, region, axis, step, half)

    def complete(now, color, region, out):
        rx, ry, rz = region
        if color == "A":
            if region == (0, 0, 0):
                for s in (1, 3, 2):
                    out.append(send(now, "A", region, "x", s))
                return
            if rz == 0 and ry == 0 and rx != FULL:
                if all(((k, 0, 0) in have["A"]) for k in (1, 2, 3)):
                    complete(now, "A", (FULL, 0, 0), out)
                return
            if rz == 0:
                if ry == 0:
                    out.append(send(now, "A", region, "y", 1))
                    out.append(send(now, "A", region, "y", 3))
                elif ry == 3:
                    out.append(send(now, "A", region, "y", 1, 0))
                elif ry == 1:
                    out.append(send(now, "A", region, "y", 3, 1))
                out.append(send(now, "A", region, "z", 1))
                out.append(send(now, "A", region, "z", 7))
            elif rz >= 5:
                out.append(send(now, "A", region, "z", 1, 0 if rz == 5 else None))
            elif rz <= 3:
                out.append(send(now, "A", region, "z", 7, 1 if rz == 3 else None))
            have["A", rz] = have.get(("A", rz), 0) + 1
            if have["A", rz] == 4:
                out.append(("sib", "A", (FULL, FULL, rz)))
            return
        mid, last = ("y", "x") if color == "B" else ("x", "y")
        m, l = AXPOS[mid], AXPOS[last]
        if region[m] != FULL and region[l] == 0:
            if region[m] == 0:
                if rz == 0:
                    out.append(send(now, color, region, "z", 1))
                    out.append(send(now, color, region, "z", 7))
                elif rz in (7, 6) or (rz == 5 and color == "B"):
                    out.append(send(now, color, region, "z", 1))
                elif rz in (1, 2) or (rz == 3 and color == "C"):
                    out.append(send(now, color, region, "z", 7))
                out.append(send(now, color, region, mid, 1))
                out.append(send(now, color, region, mid, 3))
            elif region[m] == 3 and rz % 2 == 0:
                out.append(send(now, color, region, mid, 1))
            elif region[m] == 1 and rz % 2 == 1:
                out.append(send(now, color, region, mid, 3))
            parts = []
            for k in range(4):
                r = list(region)
                r[m] = k
                parts.append(tuple(r) in have[color])
            if all(parts):
                r = list(region)
                r[m] = FULL
                complete(now, color, tuple(r), out)
            return
        if region[l] == 0:
            out.append(send(now, color, region, last, 1))
            out.append(send(now, color, region, last, 3))
        elif region[l] == 3:
            out.append(send(now, color, region, last, 1, 0))
        elif region[l] == 1:
            out.append(send(now, color, region, last, 3, 1))
        key = (color, region[l])
        have[key] = have.get(key, 0) + 1
        if have[key] == 8:
            out.append(("sib", color, (region[0], region[1], FULL)))

    first = []
    for color in "BCA":
        have[color] = {(0, 0, 0)}
        complete(0.0, color, (0, 0, 0), first)
    order.append((None, first))
    end = 0.0
    while queue:
        now, _, ident, color, region, half = heapq.heappop(queue)
        end = now
        out = []
        if half is None:
            have[color].add(region)
            complete(now, color, region, out)
        else:
            got = have[color]
            got.add((region, half))
            if (region, 1 - half) in got:
                got.add(region)
                complete(now, color, region, out)
        order.append(((ident, color, region, half), out))
    return order, count[0], end

def parts_of(ref_f, ref_r, color):
    if color == "A":
        return ref_r
    return ref_f.at[pl.ds(0 if color == "B" else PART, PART), :]


def gather_weights(wq, wo, wf, wr, send_sem, recv_sem, sib_sem, meanwhile):
    tile = lax.axis_index("tile"); group = lax.axis_index("group")
    y = tile // 8; zh = (tile // 2) % 4; c = tile % 2
    zl = group // 4; x = group % 4
    z = zh * 2 + zl

    xs = [x] + [(x + k) % 4 for k in (1, 2, 3)]
    ys = [y] + [(y + k) % 4 for k in (1, 2, 3)]
    zs = [(zl, zh)] + [(((z + k) % 8) % 2, ((z + k) % 8) // 2) for k in range(1, 8)]

    def dev_of(axis, step):
        xx, yy, zz, cc = x, y, zs[0], c
        if axis == "x": xx = xs[step]
        if axis == "y": yy = ys[step]
        if axis == "z": zz = zs[step]
        if axis == "c": cc = 1 - c
        return (yy * 8 + zz[1] * 2 + cc, zz[0] * 4 + xx)
    table = {}
    def dev(axis, step):
        if (axis, step) not in table:
            table[axis, step] = dev_of(axis, step)
        return table[axis, step]

    pack(wq, wo, group % 2, wf.at[zl, x, y, zh, c], wr.at[zl, x, y, zh, c])
    bar = pltpu.get_barrier_semaphore()
    peers = [("x", 1), ("x", 3), ("x", 2), ("y", 1), ("y", 3), ("z", 1), ("z", 7), ("c", 1)]
    for p in peers:
        pl.semaphore_signal(bar, inc=1, device_id=dev(*p), device_id_type=MESH)
    pl.semaphore_wait(bar, len(peers))

    own_f = wf.at[zl, x, y, zh, c]
    own_r = wr.at[zl, x, y, zh, c]

    def view(color, region, half=None, core=None):
        rx, ry, rz = region
        part = pl.ds(0, 4) if half is None else pl.ds(2 * half, 2)
        ix = part if rx == FULL else xs[rx]
        iy = part if ry == FULL else ys[ry]
        iz = (pl.ds(0, 2), pl.ds(0, 4)) if rz == FULL else zs[rz]
        cc = c if core is None else core
        if color == "A":
            return wr.at[iz[0], ix, iy, iz[1], cc]
        return wf.at[iz[0], ix, iy, iz[1], cc, pl.ds(0 if color == "B" else PART, PART), :]

    order, total, end = plan()
    sends, sibs = [], []
    def issue(item):
        if item[0] == "sib":
            _, color, region = item
            i = len(sibs)
            ref = view(color, region)
            cp = pltpu.make_async_remote_copy(src_ref=ref, dst_ref=ref, send_sem=sib_sem.at[0, i], recv_sem=sib_sem.at[1, i],
                                              device_id=dev("c", 1), device_id_type=MESH)
            sibs.append((cp, color, region))
        else:
            ident, color, region, axis, step, half = item
            if region == (0, 0, 0):
                ref = dst = parts_of(own_f, own_r, color)
            else:
                ref = dst = view(color, region, half)
            cp = pltpu.make_async_remote_copy(src_ref=ref, dst_ref=dst, send_sem=send_sem.at[ident], recv_sem=recv_sem.at[ident],
                                              device_id=dev(axis, step), device_id_type=MESH)
            sends.append(cp)
        cp.start()
    for n, (arrival, out) in enumerate(order):
        if arrival is not None:
            ident, color, region, half = arrival
            ref = view(color, region, half)
            pltpu.make_async_remote_copy(src_ref=ref, dst_ref=ref, send_sem=send_sem.at[ident], recv_sem=recv_sem.at[ident],
                                         device_id=dev("c", 1), device_id_type=MESH).wait_recv()
        for item in out:
            issue(item)
        if n in meanwhile:
            meanwhile[n]()
    for i, (cp, color, region) in enumerate(sibs):
        ref = view(color, region, None, 1 - c)
        pltpu.make_async_remote_copy(src_ref=ref, dst_ref=ref, send_sem=sib_sem.at[0, i], recv_sem=sib_sem.at[1, i],
                                     device_id=dev("c", 1), device_id_type=MESH).wait_recv()
    for cp in sends:
        cp.wait_send()
    for cp, _, _ in sibs:
        cp.wait_send()


def norm_block(b, index, lat, gain, xs_ref):
    quarter = D // 4
    step = lax.broadcasted_iota(jnp.int32, (8, quarter), 1).astype(jnp.float32)
    frequency = jnp.exp(step * (-math.log(10000.0) / quarter))
    side = lax.broadcasted_iota(jnp.int32, (8, quarter), 0)
    for h in range(2):
        rows = slice(b * BLOCK + h * WIN_TOK, b * BLOCK + h * WIN_TOK + WIN_TOK)
        place = index[2 * b + h]
        table = []
        for at in (lax.div(place, WIN_COLS), lax.rem(place, WIN_COLS)):
            angle = (at * WIN_SIDE + side).astype(jnp.float32) * frequency
            table.append(jnp.concatenate([jnp.sin(angle), jnp.cos(angle)], axis=1))
        tok = lat[rows, :].astype(jnp.float32)
        half = D // 2
        left = tok[:, :half].reshape(8, 8, half) + table[0][:, None, :]
        right = tok[:, half:].reshape(8, 8, half) + table[1][None]
        stream = jnp.concatenate([left.reshape(WIN_TOK, half), right.reshape(WIN_TOK, half)], axis=1)
        scale = lax.rsqrt(jnp.mean(stream * stream, axis=-1, keepdims=True) + 1e-06)
        xs_ref[rows, :] = (stream * scale * gain[...]).astype(jnp.bfloat16)


def unpack_rest(wr, wu):
    lane = lax.broadcasted_iota(jnp.int32, (PART, LANES), 1) < 64

    def one(y, carry):
        for zh in range(4):
            for c in range(2):
                for j in range(4):
                    zl, x = j // 2, (j % 2) * 2
                    even = wr[zl, x, y, zh, c].astype(jnp.float32)
                    odd = wr[zl, x + 1, y, zh, c].astype(jnp.float32)
                    low = jnp.where(lane, even, odd).astype(jnp.bfloat16)
                    high = pltpu.roll(jnp.where(lane, odd, even), 64, 1).astype(jnp.bfloat16)
                    for i in range(6):
                        wu[j, y, zh, c, 32 * i:32 * i + 16, :] = low[16 * i:16 * i + 16]
                        wu[j, y, zh, c, 32 * i + 16:32 * i + 32, :] = high[16 * i:16 * i + 16]
        return carry

    lax.fori_loop(0, 4, one, 0)


def column_tile(wf, wu, first, groups):
    spots = []
    for t, r in groups:
        spots.append((first + t // 8, (t // 2) % 4, t % 2, slice(r, r + 16)))
    tiles = []
    for k in range(12):
        j, kind = k // 3, k % 3
        if kind == 1:
            pieces = [wu[j, y, zh, c, rows, :] for y, zh, c, rows in spots]
        else:
            zl, x = j // 2, (j % 2) * 2 + kind // 2
            pieces = [wf[zl, x, y, zh, c, rows, :] for y, zh, c, rows in spots]
        tiles.append(jnp.concatenate(pieces, axis=0))
    return jnp.concatenate(tiles, axis=1)


NT = (((1,), (1,)), ((), ()))


def project(xs_ref, wf, wu, qkv):
    r = lax.broadcasted_iota(jnp.int32, (256, 256), 0) // HEAD_DIM
    c = lax.broadcasted_iota(jnp.int32, (256, 256), 1) // HEAD_DIM
    ones = jnp.where(r == c, 1.0, 0.0).astype(jnp.bfloat16)

    def half(m, carry):
        for s in range(9):
            groups = [((s * 16 + i) // 9, (s * 16 + i) % 9 * 16) for i in range(16)]
            n = 9 * m + s
            p = lax.dot_general(xs_ref[...], column_tile(wf, wu, 2 * m, groups), NT, preferred_element_type=jnp.float32)
            total = jnp.dot((p * p).astype(jnp.bfloat16), ones, preferred_element_type=jnp.float32)
            extra = jnp.where(n < 6, HEAD_DIM ** -0.5, 1.0)
            factor = jnp.where(n < 12, lax.rsqrt(total * (1.0 / HEAD_DIM) + 1e-06) * extra, 1.0)
            qkv[n] = (p * factor).astype(jnp.bfloat16)
        return carry

    lax.fori_loop(0, 2, half, 0)


def attend(qkv, lens, att):
    lane = lax.broadcasted_iota(jnp.int32, (BLOCK, LANES), 1) < 64
    key = lax.broadcasted_iota(jnp.int32, (BLOCK, 256), 1) % BLOCK
    query = lax.broadcasted_iota(jnp.int32, (BLOCK, 256), 0)
    one = jnp.where(lane, 1.0, 0.0).astype(jnp.bfloat16)
    sums = jnp.concatenate([one, 1.0 - one], axis=0).astype(jnp.bfloat16)

    def block(b, carry):
        rows = pl.ds(pl.multiple_of(b * BLOCK, BLOCK), BLOCK)
        first, second = lens[2 * b], lens[2 * b + 1]
        low = jnp.where(query < 64, 0, 64)
        high = jnp.where(query < 64, first, 64 + second)
        mask = jnp.where(key >= low, 1.0, 0.0) * jnp.where(key < high, 1.0, 0.0)

        def pair(step, inner):
            for i in range(4):
                h = 2 * step + i // 2
                part = i % 2
                cols = slice(part * LANES, part * LANES + LANES)
                q = qkv[h, rows, cols]
                k = qkv[6 + h, rows, cols]
                v = qkv[12 + h, rows, cols]
                zero = jnp.zeros_like(k)
                keys = jnp.concatenate([jnp.where(lane, k, zero), jnp.where(lane, zero, k)], axis=0)
                vals = jnp.concatenate([jnp.where(lane, v, zero), jnp.where(lane, zero, v)], axis=0)
                scores = lax.dot_general(q, keys, NT, preferred_element_type=jnp.float32)
                weights = (jnp.exp(scores) * mask).astype(jnp.bfloat16)
                mixed = jnp.dot(weights, jnp.concatenate([vals, sums], axis=1), preferred_element_type=jnp.float32)
                att[h, rows, cols] = (mixed[:, :LANES] / mixed[:, LANES:]).astype(jnp.bfloat16)
            return inner

        lax.fori_loop(0, 3, pair, 0)
        return carry

    lax.fori_loop(0, SLOTS, block, 0)


def finish(att, wf, wu, lat, lens, live, out):
    tok = lax.broadcasted_iota(jnp.int32, (BLOCK, 256), 0)

    def half(m, carry):
        for s in range(3):
            groups = [((s * 16 + i) // 3, 144 + (s * 16 + i) % 3 * 16) for i in range(16)]
            wide = jnp.concatenate([att[h] for h in range(6)], axis=1)
            update = lax.dot_general(wide, column_tile(wf, wu, 2 * m, groups), NT, preferred_element_type=jnp.float32)
            cols = pl.ds(pl.multiple_of(m * 768 + s * 256, 256), 256)
            for b in range(SLOTS):
                base = lat[b * BLOCK:(b + 1) * BLOCK, cols].astype(jnp.float32)
                first, second = lens[2 * b], lens[2 * b + 1]
                limit = jnp.where(tok < 64, first, 64 + second)
                limit = jnp.where(b < live[0], limit, 0)
                added = update[b * BLOCK:(b + 1) * BLOCK]
                out[b * BLOCK:(b + 1) * BLOCK, cols] = jnp.where(tok < limit, base + added, base).astype(jnp.bfloat16)
        return carry

    lax.fori_loop(0, 2, half, 0)


def pack(wq, wo, odd, main, rest):
    cols = jnp.concatenate([wq[...], wo[...]], axis=0).astype(jnp.float32)
    low = lax.broadcasted_iota(jnp.int32, (2 * PART, LANES), 1) < 64
    head = cols[:, :LANES]
    turned = pltpu.roll(head, 64, 1)
    last = cols[:, LANES:]
    last = jnp.concatenate([last, last], axis=1)
    pick = odd.astype(jnp.float32)
    main[...] = jnp.where(pick > 0.5, jnp.where(low, turned, last), head).astype(jnp.bfloat16)
    other = jnp.where(pick > 0.5, jnp.where(low, head, turned), last)
    side = lax.broadcasted_iota(jnp.int32, (16, LANES), 1) // 64
    for i in range(6):
        a, b = other[32 * i:32 * i + 16], other[32 * i + 16:32 * i + 32]
        rest[16 * i:16 * i + 16, :] = jnp.where(side == odd, a, b).astype(jnp.bfloat16)


WF = (2, 4, 4, 4, 2, 192, LANES)
WR = (2, 4, 4, 4, 2, PART, LANES)
WU = (4, 4, 4, 2, 192, LANES)
QKV = (18, TOK, 256)


def comm_sems():
    total = plan()[1]
    dma = pltpu.SemaphoreType.DMA
    return [dma((total,)), dma((total,)), dma((2, 16))]


def layer_kernel(index, lens, live, lat, gain, wq, wo, out, wf, wr, wu, xs, qkv, att, *sems):
    chunk = {60 + 10 * b: (lambda b=b: norm_block(b, index, lat, gain, xs)) for b in range(SLOTS)}
    gather_weights(wq, wo, wf, wr, *sems, chunk)
    unpack_rest(wr, wu)
    project(xs, wf, wu, qkv)
    attend(qkv, lens, att)
    finish(att, wf, wu, lat, lens, live, out)


def layer_call(index, lens, live, lat, gain, wq, wo):
    smem = pl.BlockSpec(memory_space=pltpu.SMEM)
    vmem = pl.BlockSpec(memory_space=pltpu.VMEM)
    bf16 = jnp.bfloat16
    return pl.pallas_call(
        layer_kernel,
        out_shape=jax.ShapeDtypeStruct((TOK, D), bf16),
        in_specs=[smem, smem, smem, vmem, vmem, vmem, vmem],
        out_specs=vmem,
        scratch_shapes=[pltpu.VMEM(WF, bf16), pltpu.VMEM(WR, bf16), pltpu.VMEM(WU, bf16), pltpu.VMEM((TOK, D), bf16),
                        pltpu.VMEM(QKV, bf16), pltpu.VMEM((6, TOK, 256), bf16)] + comm_sems(),
        compiler_params=pltpu.CompilerParams(collective_id=0, has_side_effects=True, vmem_limit_bytes=58 << 20),
    )(index, lens, live, lat, gain, wq, wo)


def local(latents, window_index, window_len, live_blocks, norm_gain, w_qkv, w_out):
    out = layer_call(window_index, window_len, live_blocks, latents.reshape(TOK, D), norm_gain.reshape(1, D),
                     w_qkv.T, w_out.T)
    return out.reshape(latents.shape)


def solution(mesh):
    in_specs = (
        P(("tile", "group"), None, None),
        P(("tile", "group")),
        P(("tile", "group")),
        P(("tile", "group")),
        P(),
        P("group", "tile"),
        P("group", "tile"),
    )
    out_specs = P(("tile", "group"), None, None)
    return jax.shard_map(local, mesh=mesh, in_specs=in_specs, out_specs=out_specs, check_vma=False)
```

```python
import math
import heapq

import jax
import jax.numpy as jnp
from jax import lax
from jax.experimental import pallas as pl
from jax.experimental.pallas import tpu as pltpu
from jax.sharding import PartitionSpec as P

D = 1536
HEAD_DIM = 64
WIN_SIDE = 8
WIN_COLS = 60
WIN_TOK = 64
SLOTS = 6
BLOCK = 128
TOK = SLOTS * BLOCK
PART = 96
LANES = 128
FULL = "F"
AXLEN = {"x": 4, "y": 4, "z": 8}
AXPOS = {"x": 0, "y": 1, "z": 2}
MESH = pl.DeviceIdType.MESH


def moved(region, axis, step):
    pos = AXPOS[axis]
    n = AXLEN[axis]
    out = list(region)
    out[pos] = (region[pos] - step) % n
    return tuple(out)

def plan():
    rate = 46.5e3
    free = {}
    queue = []
    order = []
    have = {}
    count = [0]
    seq = [0]

    def bytes_of(color, region, half):
        n = PART * 256
        for r in region:
            if r == FULL:
                n *= 4
        return n // 2 if half else n

    def send(now, color, region, axis, step, half=None):
        n = AXLEN[axis]
        hops = min(step, n - step)
        sign = 1 if step <= n // 2 else -1
        link = (axis, sign)
        start = max(now, free.get(link, 0.0))
        end = start + hops * bytes_of(color, region, half) / rate
        free[link] = end
        ident = count[0]
        count[0] += 1
        seq[0] += 1
        heapq.heappush(queue, (end + 1.0 + 0.75 * hops, seq[0], ident, color, moved(region, axis, step), half))
        return (ident, color, region, axis, step, half)

    def complete(now, color, region, out):
        rx, ry, rz = region
        if color == "A":
            if region == (0, 0, 0):
                for s in (1, 3, 2):
                    out.append(send(now, "A", region, "x", s))
                return
            if rz == 0 and ry == 0 and rx != FULL:
                if all(((k, 0, 0) in have["A"]) for k in (1, 2, 3)):
                    complete(now, "A", (FULL, 0, 0), out)
                return
            if rz == 0:
                if ry == 0:
                    out.append(send(now, "A", region, "y", 1))
                    out.append(send(now, "A", region, "y", 3))
                elif ry == 3:
                    out.append(send(now, "A", region, "y", 1, 0))
                elif ry == 1:
                    out.append(send(now, "A", region, "y", 3, 1))
                out.append(send(now, "A", region, "z", 1))
                out.append(send(now, "A", region, "z", 7))
            elif rz >= 5:
                out.append(send(now, "A", region, "z", 1, 0 if rz == 5 else None))
            elif rz <= 3:
                out.append(send(now, "A", region, "z", 7, 1 if rz == 3 else None))
            have["A", rz] = have.get(("A", rz), 0) + 1
            if have["A", rz] == 4:
                out.append(("sib", "A", (FULL, FULL, rz)))
            return
        mid, last = ("y", "x") if color == "B" else ("x", "y")
        m, l = AXPOS[mid], AXPOS[last]
        if region[m] != FULL and region[l] == 0:
            if region[m] == 0:
                if rz == 0:
                    out.append(send(now, color, region, "z", 1))
                    out.append(send(now, color, region, "z", 7))
                elif rz in (7, 6) or (rz == 5 and color == "B"):
                    out.append(send(now, color, region, "z", 1))
                elif rz in (1, 2) or (rz == 3 and color == "C"):
                    out.append(send(now, color, region, "z", 7))
                out.append(send(now, color, region, mid, 1))
                out.append(send(now, color, region, mid, 3))
            elif region[m] == 3 and rz % 2 == 0:
                out.append(send(now, color, region, mid, 1))
            elif region[m] == 1 and rz % 2 == 1:
                out.append(send(now, color, region, mid, 3))
            parts = []
            for k in range(4):
                r = list(region)
                r[m] = k
                parts.append(tuple(r) in have[color])
            if all(parts):
                r = list(region)
                r[m] = FULL
                complete(now, color, tuple(r), out)
            return
        if region[l] == 0:
            out.append(send(now, color, region, last, 1))
            out.append(send(now, color, region, last, 3))
        elif region[l] == 3:
            out.append(send(now, color, region, last, 1, 0))
        elif region[l] == 1:
            out.append(send(now, color, region, last, 3, 1))
        key = (color, region[l])
        have[key] = have.get(key, 0) + 1
        if have[key] == 8:
            out.append(("sib", color, (region[0], region[1], FULL)))

    first = []
    for color in "BCA":
        have[color] = {(0, 0, 0)}
        complete(0.0, color, (0, 0, 0), first)
    order.append((None, first))
    end = 0.0
    while queue:
        now, _, ident, color, region, half = heapq.heappop(queue)
        end = now
        out = []
        if half is None:
            have[color].add(region)
            complete(now, color, region, out)
        else:
            got = have[color]
            got.add((region, half))
            if (region, 1 - half) in got:
                got.add(region)
                complete(now, color, region, out)
        order.append(((ident, color, region, half), out))
    return order, count[0], end

def parts_of(ref_f, ref_r, color):
    if color == "A":
        return ref_r
    return ref_f.at[pl.ds(0 if color == "B" else PART, PART), :]


def gather_weights(wq, wo, wf, wr, send_sem, recv_sem, sib_sem, meanwhile):
    tile = lax.axis_index("tile"); group = lax.axis_index("group")
    y = tile // 8; zh = (tile // 2) % 4; c = tile % 2
    zl = group // 4; x = group % 4
    z = zh * 2 + zl

    xs = [x] + [(x + k) % 4 for k in (1, 2, 3)]
    ys = [y] + [(y + k) % 4 for k in (1, 2, 3)]
    zs = [(zl, zh)] + [(((z + k) % 8) % 2, ((z + k) % 8) // 2) for k in range(1, 8)]

    def dev_of(axis, step):
        xx, yy, zz, cc = x, y, zs[0], c
        if axis == "x": xx = xs[step]
        if axis == "y": yy = ys[step]
        if axis == "z": zz = zs[step]
        if axis == "c": cc = 1 - c
        return (yy * 8 + zz[1] * 2 + cc, zz[0] * 4 + xx)
    table = {}
    def dev(axis, step):
        if (axis, step) not in table:
            table[axis, step] = dev_of(axis, step)
        return table[axis, step]

    pack(wq, wo, group % 2, wf.at[zl, x, y, zh, c], wr.at[zl, x, y, zh, c])
    bar = pltpu.get_barrier_semaphore()
    peers = [("x", 1), ("x", 3), ("x", 2), ("y", 1), ("y", 3), ("z", 1), ("z", 7), ("c", 1)]
    for p in peers:
        pl.semaphore_signal(bar, inc=1, device_id=dev(*p), device_id_type=MESH)
    pl.semaphore_wait(bar, len(peers))

    own_f = wf.at[zl, x, y, zh, c]
    own_r = wr.at[zl, x, y, zh, c]

    def view(color, region, half=None, core=None):
        rx, ry, rz = region
        part = pl.ds(0, 4) if half is None else pl.ds(2 * half, 2)
        ix = part if rx == FULL else xs[rx]
        iy = part if ry == FULL else ys[ry]
        iz = (pl.ds(0, 2), pl.ds(0, 4)) if rz == FULL else zs[rz]
        cc = c if core is None else core
        if color == "A":
            return wr.at[iz[0], ix, iy, iz[1], cc]
        return wf.at[iz[0], ix, iy, iz[1], cc, pl.ds(0 if color == "B" else PART, PART), :]

    order, total, end = plan()
    sends, sibs = [], []
    def issue(item):
        if item[0] == "sib":
            _, color, region = item
            i = len(sibs)
            ref = view(color, region)
            cp = pltpu.make_async_remote_copy(src_ref=ref, dst_ref=ref, send_sem=sib_sem.at[0, i], recv_sem=sib_sem.at[1, i],
                                              device_id=dev("c", 1), device_id_type=MESH)
            sibs.append((cp, color, region))
        else:
            ident, color, region, axis, step, half = item
            if region == (0, 0, 0):
                ref = dst = parts_of(own_f, own_r, color)
            else:
                ref = dst = view(color, region, half)
            cp = pltpu.make_async_remote_copy(src_ref=ref, dst_ref=dst, send_sem=send_sem.at[ident], recv_sem=recv_sem.at[ident],
                                              device_id=dev(axis, step), device_id_type=MESH)
            sends.append(cp)
        cp.start()
    for n, (arrival, out) in enumerate(order):
        if arrival is not None:
            ident, color, region, half = arrival
            ref = view(color, region, half)
            pltpu.make_async_remote_copy(src_ref=ref, dst_ref=ref, send_sem=send_sem.at[ident], recv_sem=recv_sem.at[ident],
                                         device_id=dev("c", 1), device_id_type=MESH).wait_recv()
        for item in out:
            issue(item)
        if n in meanwhile:
            meanwhile[n]()
    for i, (cp, color, region) in enumerate(sibs):
        ref = view(color, region, None, 1 - c)
        pltpu.make_async_remote_copy(src_ref=ref, dst_ref=ref, send_sem=sib_sem.at[0, i], recv_sem=sib_sem.at[1, i],
                                     device_id=dev("c", 1), device_id_type=MESH).wait_recv()
    for cp in sends:
        cp.wait_send()
    for cp, _, _ in sibs:
        cp.wait_send()


def norm_block(b, index, lat, gain, xs_ref):
    quarter = D // 4
    step = lax.broadcasted_iota(jnp.int32, (8, quarter), 1).astype(jnp.float32)
    frequency = jnp.exp(step * (-math.log(10000.0) / quarter))
    side = lax.broadcasted_iota(jnp.int32, (8, quarter), 0)
    for h in range(2):
        rows = pl.ds(pl.multiple_of(b * BLOCK + h * WIN_TOK, WIN_TOK), WIN_TOK)
        place = index[2 * b + h]
        table = []
        for at in (lax.div(place, WIN_COLS), lax.rem(place, WIN_COLS)):
            angle = (at * WIN_SIDE + side).astype(jnp.float32) * frequency
            table.append(jnp.concatenate([jnp.sin(angle), jnp.cos(angle)], axis=1))
        tok = lat[rows, :].astype(jnp.float32)
        half = D // 2
        left = tok[:, :half].reshape(8, 8, half) + table[0][:, None, :]
        right = tok[:, half:].reshape(8, 8, half) + table[1][None]
        stream = jnp.concatenate([left.reshape(WIN_TOK, half), right.reshape(WIN_TOK, half)], axis=1)
        scale = lax.rsqrt(jnp.mean(stream * stream, axis=-1, keepdims=True) + 1e-06)
        wide = jnp.concatenate([gain[k:k + 1, :] for k in range(D // LANES)], axis=1)
        xs_ref[rows, :] = (stream * scale * wide).astype(jnp.bfloat16)


def unpack_rest(wr, wu):
    lane = lax.broadcasted_iota(jnp.int32, (PART, LANES), 1) < 64

    def one(y, carry):
        for zh in range(4):
            for c in range(2):
                for j in range(4):
                    zl, x = j // 2, (j % 2) * 2
                    even = wr[zl, x, y, zh, c].astype(jnp.float32)
                    odd = wr[zl, x + 1, y, zh, c].astype(jnp.float32)
                    low = jnp.where(lane, even, odd).astype(jnp.bfloat16)
                    high = pltpu.roll(jnp.where(lane, odd, even), 64, 1).astype(jnp.bfloat16)
                    for i in range(6):
                        wu[j, y, zh, c, 32 * i:32 * i + 16, :] = low[16 * i:16 * i + 16]
                        wu[j, y, zh, c, 32 * i + 16:32 * i + 32, :] = high[16 * i:16 * i + 16]
        return carry

    lax.fori_loop(0, 4, one, 0)


def column_tile(wf, wu, first, groups):
    spots = []
    for t, r in groups:
        if isinstance(t, int):
            spots.append((first + t // 8, (t // 2) % 4, t % 2, slice(r, r + 16)))
        else:
            half = lax.div(t, 2)
            y = lax.div(t, 8)
            spots.append((y, half - 4 * y, t - 2 * half, pl.ds(pl.multiple_of(r, 16), 16)))
    tiles = []
    for k in range(12):
        j, kind = k // 3, k % 3
        if kind == 1:
            pieces = [wu[j, y, zh, c, rows, :] for y, zh, c, rows in spots]
        else:
            zl, x = j // 2, (j % 2) * 2 + kind // 2
            pieces = [wf[zl, x, y, zh, c, rows, :] for y, zh, c, rows in spots]
        tiles.append(jnp.concatenate(pieces, axis=0))
    return jnp.concatenate(tiles, axis=1)


NT = (((1,), (1,)), ((), ()))


def project(xs_ref, wf, wu, qkv):
    r = lax.broadcasted_iota(jnp.int32, (256, 256), 0) // HEAD_DIM
    c = lax.broadcasted_iota(jnp.int32, (256, 256), 1) // HEAD_DIM
    ones = jnp.where(r == c, 1.0, 0.0).astype(jnp.bfloat16)

    def tile(n, carry):
        t0 = lax.div(16 * n, 9)
        r0 = 16 * n - 9 * t0
        groups = []
        for i in range(16):
            r = r0 + i
            over = (r >= 9).astype(jnp.int32) + (r >= 18).astype(jnp.int32)
            groups.append((t0 + over, 16 * (r - 9 * over)))
        p = lax.dot_general(xs_ref[...], column_tile(wf, wu, 0, groups), NT, preferred_element_type=jnp.float32)
        total = jnp.dot((p * p).astype(jnp.bfloat16), ones, preferred_element_type=jnp.float32)
        extra = jnp.where(n < 6, HEAD_DIM ** -0.5, 1.0)
        factor = jnp.where(n < 12, lax.rsqrt(total * (1.0 / HEAD_DIM) + 1e-06) * extra, 1.0)
        qkv[n] = (p * factor).astype(jnp.bfloat16)
        return carry

    lax.fori_loop(0, 18, tile, 0)


def attend(qkv, lens, att):
    lane = lax.broadcasted_iota(jnp.int32, (BLOCK, LANES), 1) < 64
    key = lax.broadcasted_iota(jnp.int32, (BLOCK, 256), 1) % BLOCK
    query = lax.broadcasted_iota(jnp.int32, (BLOCK, 256), 0)
    one = jnp.where(lane, 1.0, 0.0).astype(jnp.bfloat16)
    sums = jnp.concatenate([one, 1.0 - one], axis=0).astype(jnp.bfloat16)

    def block(b, carry):
        rows = pl.ds(pl.multiple_of(b * BLOCK, BLOCK), BLOCK)
        first, second = lens[2 * b], lens[2 * b + 1]
        low = jnp.where(query < 64, 0, 64)
        high = jnp.where(query < 64, first, 64 + second)
        mask = jnp.where(key >= low, 1.0, 0.0) * jnp.where(key < high, 1.0, 0.0)

        def pair(step, inner):
            for i in range(4):
                h = 2 * step + i // 2
                part = i % 2
                cols = slice(part * LANES, part * LANES + LANES)
                q = qkv[h, rows, cols]
                k = qkv[6 + h, rows, cols]
                v = qkv[12 + h, rows, cols]
                zero = jnp.zeros_like(k)
                keys = jnp.concatenate([jnp.where(lane, k, zero), jnp.where(lane, zero, k)], axis=0)
                vals = jnp.concatenate([jnp.where(lane, v, zero), jnp.where(lane, zero, v)], axis=0)
                scores = lax.dot_general(q, keys, NT, preferred_element_type=jnp.float32)
                weights = (jnp.exp(scores) * mask).astype(jnp.bfloat16)
                mixed = jnp.dot(weights, jnp.concatenate([vals, sums], axis=1), preferred_element_type=jnp.float32)
                att[h, rows, cols] = (mixed[:, :LANES] / mixed[:, LANES:]).astype(jnp.bfloat16)
            return inner

        lax.fori_loop(0, 3, pair, 0)
        return carry

    lax.fori_loop(0, SLOTS, block, 0)


def finish(att, wf, wu, lat, lens, live, out):
    tok = lax.broadcasted_iota(jnp.int32, (BLOCK, 256), 0)

    def half(m, carry):
        for s in range(3):
            groups = [((s * 16 + i) // 3, 144 + (s * 16 + i) % 3 * 16) for i in range(16)]
            wide = jnp.concatenate([att[h] for h in range(6)], axis=1)
            update = lax.dot_general(wide, column_tile(wf, wu, 2 * m, groups), NT, preferred_element_type=jnp.float32)
            cols = pl.ds(pl.multiple_of(m * 768 + s * 256, 256), 256)
            for b in range(SLOTS):
                base = lat[b * BLOCK:(b + 1) * BLOCK, cols].astype(jnp.float32)
                first, second = lens[2 * b], lens[2 * b + 1]
                limit = jnp.where(tok < 64, first, 64 + second)
                limit = jnp.where(b < live[0], limit, 0)
                added = update[b * BLOCK:(b + 1) * BLOCK]
                out[b * BLOCK:(b + 1) * BLOCK, cols] = jnp.where(tok < limit, base + added, base).astype(jnp.bfloat16)
        return carry

    lax.fori_loop(0, 2, half, 0)


def pack(wq, wo, odd, main, rest):
    cols = jnp.concatenate([wq[...], wo[...]], axis=0).astype(jnp.float32)
    low = lax.broadcasted_iota(jnp.int32, (2 * PART, LANES), 1) < 64
    head = cols[:, :LANES]
    turned = pltpu.roll(head, 64, 1)
    last = cols[:, LANES:]
    last = jnp.concatenate([last, last], axis=1)
    pick = odd.astype(jnp.float32)
    main[...] = jnp.where(pick > 0.5, jnp.where(low, turned, last), head).astype(jnp.bfloat16)
    other = jnp.where(pick > 0.5, jnp.where(low, head, turned), last)
    side = lax.broadcasted_iota(jnp.int32, (16, LANES), 1) // 64
    for i in range(6):
        a, b = other[32 * i:32 * i + 16], other[32 * i + 16:32 * i + 32]
        rest[16 * i:16 * i + 16, :] = jnp.where(side == odd, a, b).astype(jnp.bfloat16)


WF = (2, 4, 4, 4, 2, 192, LANES)
WR = (2, 4, 4, 4, 2, PART, LANES)
WU = (4, 4, 4, 2, 192, LANES)
QKV = (18, TOK, 256)


def comm_sems():
    total = plan()[1]
    dma = pltpu.SemaphoreType.DMA
    return [dma((total,)), dma((total,)), dma((2, 16))]


def norm_tokens(index, lat, gain, xs):
    def block(b, carry):
        norm_block(b, index, lat, gain, xs)
        return carry

    lax.fori_loop(0, SLOTS, block, 0)


def layer_kernel(index, lens, live, lat_hbm, gain, wq, wo, out, wf, wr, wu, xs, qkv, att, lat, lat_sem, *sems):
    fetch = pltpu.make_async_copy(lat_hbm, lat, lat_sem)
    fetch.start()
    chunk = {50: fetch.wait, 100: lambda: norm_tokens(index, lat, gain, xs)}
    gather_weights(wq, wo, wf, wr, *sems, chunk)
    unpack_rest(wr, wu)
    project(xs, wf, wu, qkv)
    attend(qkv, lens, att)
    finish(att, wf, wu, lat, lens, live, out)


def layer_call(index, lens, live, lat, gain, wq, wo):
    smem = pl.BlockSpec(memory_space=pltpu.SMEM)
    vmem = pl.BlockSpec(memory_space=pltpu.VMEM)
    bf16 = jnp.bfloat16
    return pl.pallas_call(
        layer_kernel,
        out_shape=pltpu.VMEM((TOK, D), bf16),
        in_specs=[smem, smem, smem, pl.BlockSpec(memory_space=pl.ANY), vmem, vmem, vmem],
        out_specs=vmem,
        scratch_shapes=[pltpu.VMEM(WF, bf16), pltpu.VMEM(WR, bf16), pltpu.VMEM(WU, bf16), pltpu.VMEM((TOK, D), bf16),
                        pltpu.VMEM(QKV, bf16), pltpu.VMEM((6, TOK, 256), bf16),
                        pltpu.VMEM((TOK, D), bf16), pltpu.SemaphoreType.DMA] + comm_sems(),
        compiler_params=pltpu.CompilerParams(collective_id=0, has_side_effects=True, vmem_limit_bytes=58 << 20),
    )(index, lens, live, lat, gain, wq, wo)


def local(latents, window_index, window_len, live_blocks, norm_gain, w_qkv, w_out):
    out = layer_call(window_index, window_len, live_blocks, latents.reshape(TOK, D), norm_gain.reshape(D // LANES, LANES),
                     w_qkv.T, w_out.T)
    return out.reshape(latents.shape)


def solution(mesh):
    in_specs = (
        P(("tile", "group"), None, None),
        P(("tile", "group")),
        P(("tile", "group")),
        P(("tile", "group")),
        P(),
        P("group", "tile"),
        P("group", "tile"),
    )
    out_specs = P(("tile", "group"), None, None)
    return jax.shard_map(local, mesh=mesh, in_specs=in_specs, out_specs=out_specs, check_vma=False)
```

```python
import math
import heapq

import jax
import jax.numpy as jnp
from jax import lax
from jax.experimental import pallas as pl
from jax.experimental.pallas import tpu as pltpu
from jax.sharding import PartitionSpec as P

D = 1536
HEAD_DIM = 64
WIN_SIDE = 8
WIN_COLS = 60
WIN_TOK = 64
SLOTS = 6
BLOCK = 128
TOK = SLOTS * BLOCK
PART = 96
LANES = 128
FULL = "F"
AXLEN = {"x": 4, "y": 4, "z": 8}
AXPOS = {"x": 0, "y": 1, "z": 2}
MESH = pl.DeviceIdType.MESH


def moved(region, axis, step):
    pos = AXPOS[axis]
    n = AXLEN[axis]
    out = list(region)
    out[pos] = (region[pos] - step) % n
    return tuple(out)

def plan():
    rate = 46.5e3
    free = {}
    queue = []
    order = []
    have = {}
    count = [0]
    seq = [0]

    def bytes_of(color, region, half):
        n = PART * 256
        for r in region:
            if r == FULL:
                n *= 4
        return n if half is None else n // 2

    def send(now, color, region, axis, step, half=None):
        n = AXLEN[axis]
        hops = min(step, n - step)
        sign = 1 if step <= n // 2 else -1
        link = (axis, sign)
        start = max(now, free.get(link, 0.0))
        end = start + hops * bytes_of(color, region, half) / rate
        free[link] = end
        ident = count[0]
        count[0] += 1
        seq[0] += 1
        heapq.heappush(queue, (end + 2.2 + 0.75 * hops, seq[0], ident, color, moved(region, axis, step), half))
        return (ident, color, region, axis, step, half)

    def complete(now, color, region, out):
        rx, ry, rz = region
        if color == "A":
            if region == (0, 0, 0):
                for s in (1, 3, 2):
                    out.append(send(now, "A", region, "x", s))
                return
            if rz == 0 and ry == 0 and rx != FULL:
                if all(((k, 0, 0) in have["A"]) for k in (1, 2, 3)):
                    complete(now, "A", (FULL, 0, 0), out)
                return
            if rz == 0:
                if ry == 0:
                    out.append(send(now, "A", region, "y", 1))
                    out.append(send(now, "A", region, "y", 3))
                elif ry == 3:
                    out.append(send(now, "A", region, "y", 1, 0))
                elif ry == 1:
                    out.append(send(now, "A", region, "y", 3, 1))
                out.append(send(now, "A", region, "z", 1))
                out.append(send(now, "A", region, "z", 7))
            elif rz >= 5:
                out.append(send(now, "A", region, "z", 1, 0 if rz == 5 else None))
            elif rz <= 3:
                out.append(send(now, "A", region, "z", 7, 1 if rz == 3 else None))
            have["A", rz] = have.get(("A", rz), 0) + 1
            if have["A", rz] == 4:
                out.append(("sib", "A", (FULL, FULL, rz)))
            return
        mid, last = ("y", "x") if color == "B" else ("x", "y")
        m, l = AXPOS[mid], AXPOS[last]
        if region[m] != FULL and region[l] == 0:
            if region[m] == 0:
                if rz == 0:
                    out.append(send(now, color, region, "z", 1))
                    out.append(send(now, color, region, "z", 7))
                elif rz in (7, 6) or (rz == 5 and color == "B"):
                    out.append(send(now, color, region, "z", 1))
                elif rz in (1, 2) or (rz == 3 and color == "C"):
                    out.append(send(now, color, region, "z", 7))
                out.append(send(now, color, region, mid, 1))
                out.append(send(now, color, region, mid, 3))
            elif region[m] == 3 and rz % 2 == 0:
                out.append(send(now, color, region, mid, 1))
            elif region[m] == 1 and rz % 2 == 1:
                out.append(send(now, color, region, mid, 3))
            parts = []
            for k in range(4):
                r = list(region)
                r[m] = k
                parts.append(tuple(r) in have[color])
            if all(parts):
                r = list(region)
                r[m] = FULL
                complete(now, color, tuple(r), out)
            return
        if region[l] == 0:
            out.append(send(now, color, region, last, 1))
            out.append(send(now, color, region, last, 3))
        elif region[l] == 3:
            out.append(send(now, color, region, last, 1, 0))
        elif region[l] == 1:
            out.append(send(now, color, region, last, 3, 1))
        key = (color, region[l])
        have[key] = have.get(key, 0) + 1
        if region[l] == 2:
            out.append(("sib", color, region))
        elif have[key] == 8:
            out.append(("sib", color, (region[0], region[1], FULL)))

    first = []
    for color in "BCA":
        have[color] = {(0, 0, 0)}
        complete(0.0, color, (0, 0, 0), first)
    order.append((None, first))
    end = 0.0
    while queue:
        now, _, ident, color, region, half = heapq.heappop(queue)
        end = now
        out = []
        if half is None:
            have[color].add(region)
            complete(now, color, region, out)
        else:
            got = have[color]
            got.add((region, half))
            if (region, 1 - half) in got:
                got.add(region)
                complete(now, color, region, out)
        order.append(((ident, color, region, half), out))
    return order, count[0], end

def parts_of(ref_f, ref_r, color):
    if color == "A":
        return ref_r
    return ref_f.at[pl.ds(0 if color == "B" else PART, PART), :]


def gather_weights(wq, wo, wf, wr, send_sem, recv_sem, sib_sem, meanwhile):
    tile = lax.axis_index("tile"); group = lax.axis_index("group")
    y = tile // 8; zh = (tile // 2) % 4; c = tile % 2
    zl = group // 4; x = group % 4
    z = zh * 2 + zl

    xs = [x] + [(x + k) % 4 for k in (1, 2, 3)]
    ys = [y] + [(y + k) % 4 for k in (1, 2, 3)]
    zs = [(zl, zh)] + [(((z + k) % 8) % 2, ((z + k) % 8) // 2) for k in range(1, 8)]

    def dev_of(axis, step):
        xx, yy, zz, cc = x, y, zs[0], c
        if axis == "x": xx = xs[step]
        if axis == "y": yy = ys[step]
        if axis == "z": zz = zs[step]
        if axis == "c": cc = 1 - c
        return (yy * 8 + zz[1] * 2 + cc, zz[0] * 4 + xx)
    table = {}
    def dev(axis, step):
        if (axis, step) not in table:
            table[axis, step] = dev_of(axis, step)
        return table[axis, step]

    pack(wq, wo, group % 2, wf.at[zl, x, y, zh, c], wr.at[zl, x, y, zh, c])
    bar = pltpu.get_barrier_semaphore()
    peers = [("x", 1), ("x", 3), ("x", 2), ("y", 1), ("y", 3), ("z", 1), ("z", 7), ("c", 1)]
    for p in peers:
        pl.semaphore_signal(bar, inc=1, device_id=dev(*p), device_id_type=MESH)
    pl.semaphore_wait(bar, len(peers))

    own_f = wf.at[zl, x, y, zh, c]
    own_r = wr.at[zl, x, y, zh, c]

    def view(color, region, half=None, core=None):
        rx, ry, rz = region
        part = pl.ds(0, 4) if half is None else pl.ds(2 * half, 2)
        ix = part if rx == FULL else xs[rx]
        iy = part if ry == FULL else ys[ry]
        iz = (pl.ds(0, 2), pl.ds(0, 4)) if rz == FULL else zs[rz]
        cc = c if core is None else core
        if color == "A":
            return wr.at[iz[0], ix, iy, iz[1], cc]
        return wf.at[iz[0], ix, iy, iz[1], cc, pl.ds(0 if color == "B" else PART, PART), :]

    order, total, end = plan()
    sends, sibs = [], []
    def issue(item):
        if item[0] == "sib":
            _, color, region = item
            i = len(sibs)
            ref = view(color, region)
            cp = pltpu.make_async_remote_copy(src_ref=ref, dst_ref=ref, send_sem=sib_sem.at[0, i], recv_sem=sib_sem.at[1, i],
                                              device_id=dev("c", 1), device_id_type=MESH)
            sibs.append((cp, color, region))
        else:
            ident, color, region, axis, step, half = item
            if region == (0, 0, 0):
                ref = dst = parts_of(own_f, own_r, color)
            else:
                ref = dst = view(color, region, half)
            cp = pltpu.make_async_remote_copy(src_ref=ref, dst_ref=dst, send_sem=send_sem.at[ident], recv_sem=recv_sem.at[ident],
                                              device_id=dev(axis, step), device_id_type=MESH)
            sends.append(cp)
        cp.start()
    for n, (arrival, out) in enumerate(order):
        if arrival is not None:
            ident, color, region, half = arrival
            ref = view(color, region, half)
            pltpu.make_async_remote_copy(src_ref=ref, dst_ref=ref, send_sem=send_sem.at[ident], recv_sem=recv_sem.at[ident],
                                         device_id=dev("c", 1), device_id_type=MESH).wait_recv()
        for item in out:
            issue(item)
        if n in meanwhile:
            meanwhile[n]()
    for i, (cp, color, region) in enumerate(sibs):
        ref = view(color, region, None, 1 - c)
        pltpu.make_async_remote_copy(src_ref=ref, dst_ref=ref, send_sem=sib_sem.at[0, i], recv_sem=sib_sem.at[1, i],
                                     device_id=dev("c", 1), device_id_type=MESH).wait_recv()
    return sends + [cp for cp, _, _ in sibs]


def norm_block(b, index, lat, gain, xs_ref):
    quarter = D // 4
    step = lax.broadcasted_iota(jnp.int32, (8, quarter), 1).astype(jnp.float32)
    frequency = jnp.exp(step * (-math.log(10000.0) / quarter))
    side = lax.broadcasted_iota(jnp.int32, (8, quarter), 0)
    for h in range(2):
        rows = pl.ds(pl.multiple_of(b * BLOCK + h * WIN_TOK, WIN_TOK), WIN_TOK)
        place = index[2 * b + h]
        table = []
        for at in (lax.div(place, WIN_COLS), lax.rem(place, WIN_COLS)):
            angle = (at * WIN_SIDE + side).astype(jnp.float32) * frequency
            table.append(jnp.concatenate([jnp.sin(angle), jnp.cos(angle)], axis=1))
        tok = lat[rows, :].astype(jnp.float32)
        half = D // 2
        left = tok[:, :half].reshape(8, 8, half) + table[0][:, None, :]
        right = tok[:, half:].reshape(8, 8, half) + table[1][None]
        stream = jnp.concatenate([left.reshape(WIN_TOK, half), right.reshape(WIN_TOK, half)], axis=1)
        scale = lax.rsqrt(jnp.mean(stream * stream, axis=-1, keepdims=True) + 1e-06)
        wide = jnp.concatenate([gain[k:k + 1, :] for k in range(D // LANES)], axis=1)
        xs_ref[rows, :] = (stream * scale * wide).astype(jnp.bfloat16)


def unpack_rest(wr, wu):
    lane = lax.broadcasted_iota(jnp.int32, (PART, LANES), 1) < 64

    def one(y, carry):
        for zh in range(4):
            for c in range(2):
                for j in range(4):
                    zl, x = j // 2, (j % 2) * 2
                    even = wr[zl, x, y, zh, c].astype(jnp.float32)
                    odd = wr[zl, x + 1, y, zh, c].astype(jnp.float32)
                    low = jnp.where(lane, even, odd).astype(jnp.bfloat16)
                    high = pltpu.roll(jnp.where(lane, odd, even), 64, 1).astype(jnp.bfloat16)
                    for i in range(6):
                        wu[j, y, zh, c, 32 * i:32 * i + 16, :] = low[16 * i:16 * i + 16]
                        wu[j, y, zh, c, 32 * i + 16:32 * i + 32, :] = high[16 * i:16 * i + 16]
        return carry

    lax.fori_loop(0, 4, one, 0)


def column_tile(wf, wu, first, groups):
    spots = []
    for t, r in groups:
        if isinstance(t, int):
            spots.append((first + t // 8, (t // 2) % 4, t % 2, slice(r, r + 16)))
        else:
            half = lax.div(t, 2)
            y = lax.div(t, 8)
            spots.append((y, half - 4 * y, t - 2 * half, pl.ds(pl.multiple_of(r, 16), 16)))
    tiles = []
    for k in range(12):
        j, kind = k // 3, k % 3
        if kind == 1:
            pieces = [wu[j, y, zh, c, rows, :] for y, zh, c, rows in spots]
        else:
            zl, x = j // 2, (j % 2) * 2 + kind // 2
            pieces = [wf[zl, x, y, zh, c, rows, :] for y, zh, c, rows in spots]
        tiles.append(jnp.concatenate(pieces, axis=0))
    return jnp.concatenate(tiles, axis=1)


NT = (((1,), (1,)), ((), ()))


def project(xs_ref, wf, wu, qkv):
    r = lax.broadcasted_iota(jnp.int32, (256, 256), 0) // HEAD_DIM
    c = lax.broadcasted_iota(jnp.int32, (256, 256), 1) // HEAD_DIM
    ones = jnp.where(r == c, 1.0, 0.0).astype(jnp.bfloat16)

    def tile(n, carry):
        t0 = lax.div(16 * n, 9)
        r0 = 16 * n - 9 * t0
        groups = []
        for i in range(16):
            r = r0 + i
            over = (r >= 9).astype(jnp.int32) + (r >= 18).astype(jnp.int32)
            groups.append((t0 + over, 16 * (r - 9 * over)))
        p = lax.dot_general(xs_ref[...], column_tile(wf, wu, 0, groups), NT, preferred_element_type=jnp.float32)
        total = jnp.dot((p * p).astype(jnp.bfloat16), ones, preferred_element_type=jnp.float32)
        extra = jnp.where(n < 6, HEAD_DIM ** -0.5, 1.0)
        factor = jnp.where(n < 12, lax.rsqrt(total * (1.0 / HEAD_DIM) + 1e-06) * extra, 1.0)
        qkv[n] = (p * factor).astype(jnp.bfloat16)
        return carry

    lax.fori_loop(0, 18, tile, 0)


def attend(qkv, lens, att):
    lane = lax.broadcasted_iota(jnp.int32, (BLOCK, LANES), 1) < 64
    key = lax.broadcasted_iota(jnp.int32, (BLOCK, 256), 1) % BLOCK
    query = lax.broadcasted_iota(jnp.int32, (BLOCK, 256), 0)
    one = jnp.where(lane, 1.0, 0.0).astype(jnp.bfloat16)
    sums = jnp.concatenate([one, 1.0 - one], axis=0).astype(jnp.bfloat16)

    def block(b, carry):
        rows = pl.ds(pl.multiple_of(b * BLOCK, BLOCK), BLOCK)
        first, second = lens[2 * b], lens[2 * b + 1]
        low = jnp.where(query < 64, 0, 64)
        high = jnp.where(query < 64, first, 64 + second)
        mask = jnp.where(key >= low, 1.0, 0.0) * jnp.where(key < high, 1.0, 0.0)

        def pair(step, inner):
            for i in range(4):
                h = 2 * step + i // 2
                part = i % 2
                cols = slice(part * LANES, part * LANES + LANES)
                q = qkv[h, rows, cols]
                k = qkv[6 + h, rows, cols]
                v = qkv[12 + h, rows, cols]
                zero = jnp.zeros_like(k)
                keys = jnp.concatenate([jnp.where(lane, k, zero), jnp.where(lane, zero, k)], axis=0)
                vals = jnp.concatenate([jnp.where(lane, v, zero), jnp.where(lane, zero, v)], axis=0)
                scores = lax.dot_general(q, keys, NT, preferred_element_type=jnp.float32)
                weights = (jnp.exp(scores) * mask).astype(jnp.bfloat16)
                mixed = jnp.dot(weights, jnp.concatenate([vals, sums], axis=1), preferred_element_type=jnp.float32)
                att[h, rows, cols] = (mixed[:, :LANES] / mixed[:, LANES:]).astype(jnp.bfloat16)
            return inner

        lax.fori_loop(0, 3, pair, 0)
        return carry

    lax.fori_loop(0, SLOTS, block, 0)


def finish(att, wf, wu, lat, lens, live, out):
    tok = lax.broadcasted_iota(jnp.int32, (BLOCK, 256), 0)

    def half(m, carry):
        for s in range(3):
            groups = [((s * 16 + i) // 3, 144 + (s * 16 + i) % 3 * 16) for i in range(16)]
            wide = jnp.concatenate([att[h] for h in range(6)], axis=1)
            update = lax.dot_general(wide, column_tile(wf, wu, 2 * m, groups), NT, preferred_element_type=jnp.float32)
            cols = pl.ds(pl.multiple_of(m * 768 + s * 256, 256), 256)
            for b in range(SLOTS):
                base = lat[b * BLOCK:(b + 1) * BLOCK, cols].astype(jnp.float32)
                first, second = lens[2 * b], lens[2 * b + 1]
                limit = jnp.where(tok < 64, first, 64 + second)
                limit = jnp.where(b < live[0], limit, 0)
                added = update[b * BLOCK:(b + 1) * BLOCK]
                out[b * BLOCK:(b + 1) * BLOCK, cols] = jnp.where(tok < limit, base + added, base).astype(jnp.bfloat16)
        return carry

    lax.fori_loop(0, 2, half, 0)


def pack(wq, wo, odd, main, rest):
    cols = jnp.concatenate([wq[...], wo[...]], axis=0).astype(jnp.float32)
    low = lax.broadcasted_iota(jnp.int32, (2 * PART, LANES), 1) < 64
    head = cols[:, :LANES]
    turned = pltpu.roll(head, 64, 1)
    last = cols[:, LANES:]
    last = jnp.concatenate([last, last], axis=1)
    pick = odd.astype(jnp.float32)
    main[...] = jnp.where(pick > 0.5, jnp.where(low, turned, last), head).astype(jnp.bfloat16)
    other = jnp.where(pick > 0.5, jnp.where(low, head, turned), last)
    side = lax.broadcasted_iota(jnp.int32, (16, LANES), 1) // 64
    for i in range(6):
        a, b = other[32 * i:32 * i + 16], other[32 * i + 16:32 * i + 32]
        rest[16 * i:16 * i + 16, :] = jnp.where(side == odd, a, b).astype(jnp.bfloat16)


WF = (2, 4, 4, 4, 2, 192, LANES)
WR = (2, 4, 4, 4, 2, PART, LANES)
WU = (4, 4, 4, 2, 192, LANES)
QKV = (18, TOK, 256)


def comm_sems():
    total = plan()[1]
    dma = pltpu.SemaphoreType.DMA
    return [dma((total,)), dma((total,)), dma((2, 32))]


def norm_tokens(index, lat, gain, xs):
    def block(b, carry):
        norm_block(b, index, lat, gain, xs)
        return carry

    lax.fori_loop(0, SLOTS, block, 0)


def layer_kernel(index, lens, live, lat_hbm, gain, wq, wo, out, wf, wr, wu, xs, qkv, att, lat, lat_sem, *sems):
    fetch = pltpu.make_async_copy(lat_hbm, lat, lat_sem)
    fetch.start()
    chunk = {50: fetch.wait, 100: lambda: norm_tokens(index, lat, gain, xs)}
    sent = gather_weights(wq, wo, wf, wr, *sems, chunk)
    unpack_rest(wr, wu)
    project(xs, wf, wu, qkv)
    attend(qkv, lens, att)
    finish(att, wf, wu, lat, lens, live, out)
    for cp in sent:
        cp.wait_send()


def layer_call(index, lens, live, lat, gain, wq, wo):
    smem = pl.BlockSpec(memory_space=pltpu.SMEM)
    vmem = pl.BlockSpec(memory_space=pltpu.VMEM)
    bf16 = jnp.bfloat16
    return pl.pallas_call(
        layer_kernel,
        out_shape=pltpu.VMEM((TOK, D), bf16),
        in_specs=[smem, smem, smem, pl.BlockSpec(memory_space=pl.ANY), vmem, vmem, vmem],
        out_specs=vmem,
        scratch_shapes=[pltpu.VMEM(WF, bf16), pltpu.VMEM(WR, bf16), pltpu.VMEM(WU, bf16), pltpu.VMEM((TOK, D), bf16),
                        pltpu.VMEM(QKV, bf16), pltpu.VMEM((6, TOK, 256), bf16),
                        pltpu.VMEM((TOK, D), bf16), pltpu.SemaphoreType.DMA] + comm_sems(),
        compiler_params=pltpu.CompilerParams(collective_id=0, has_side_effects=True, vmem_limit_bytes=58 << 20),
    )(index, lens, live, lat, gain, wq, wo)


def local(latents, window_index, window_len, live_blocks, norm_gain, w_qkv, w_out):
    out = layer_call(window_index, window_len, live_blocks, latents.reshape(TOK, D), norm_gain.reshape(D // LANES, LANES),
                     w_qkv.T, w_out.T)
    return out.reshape(latents.shape)


def solution(mesh):
    in_specs = (
        P(("tile", "group"), None, None),
        P(("tile", "group")),
        P(("tile", "group")),
        P(("tile", "group")),
        P(),
        P("group", "tile"),
        P("group", "tile"),
    )
    out_specs = P(("tile", "group"), None, None)
    return jax.shard_map(local, mesh=mesh, in_specs=in_specs, out_specs=out_specs, check_vma=False)
```
